32 devices in a mesh: replica: 2 (over y), shard: 16 (over z, x, core).
Axes of the slice: x: 2, y: 2, z: 4, core: 2. Of those that a mesh axis runs over, the one named last changes fastest.
Arguments:
- hidden_states: bfloat16 [8192, 7168], P(('replica', 'shard')), may hold values from -6 to 6
- latent_grad: bfloat16 [8192, 512], P(('replica', 'shard')), may hold values from -0.15625 to 0.15625
- left_factor: float32 [80, 256, 256], P('shard', 'replica'), may hold values from -2 to 45, as said below
- right_factor: float32 [80, 256, 256], P('shard', 'replica'), may hold values from -2 to 45, as said below
- left_root: bfloat16 [80, 256, 256], P('shard'), may hold values from -1 to 4, as said below
- right_root: bfloat16 [80, 256, 256], P('shard'), may hold values from -1 to 4, as said below
- block_owner: int32 [56], replicated, may hold values from 0 to 15, as said below
- block_slot: int32 [56], replicated, may hold values from 0 to 4, as said below
Outputs:
- new_left: float32 [80, 256, 256], P('shard', 'replica')
- new_right: float32 [80, 256, 256], P('shard', 'replica')
- update: float32 [2, 256, 7168], P(None, 'shard')
The draws below stay inside these ranges and needn't reach their ends.
Inputs may be any that keep to these rules, and one draw needn't show every extreme that they name: `block_owner`: no owner holds more than 5 blocks, and some owner holds exactly 5. `block_slot`: no two blocks have both the same owner and the same slot. `left_factor`: Symmetric. `right_factor`: Symmetric. `left_root`: Symmetric. `right_root`: Symmetric.
All inputs are finite; a program needn't handle non-finite values.
Results may differ from the reference program's by a relative error of at most 0.005.
Values may be sent and summed in bfloat16 or wider, within the bound.
No kernel may reach another device: no remote copies, remote signals or barrier semaphores. Data moves between devices by JAX's collectives and lax.ppermute only.
A program may use at most 64 MiB of HBM per device.

```python
import math
import jax
import jax.numpy as jnp
from jax import lax

D = 7168
LAT = 512
BS = 256
TOK_DEV = 256
TOKENS = 8192
CAP = 5
N_REPLICA = 2
N_SHARD = 16


def plan_arrays(key):
    total_blocks = LAT // BS * (D // BS)
    positions = jnp.arange(total_blocks, dtype=jnp.int32)
    leading = positions < CAP
    owner_rank = jnp.where(leading, 0, 1 + (positions - CAP) % (N_SHARD - 1))
    slot_index = jnp.where(leading, positions, (positions - CAP) // (N_SHARD - 1))
    owner_perm = jax.random.permutation(jax.random.fold_in(key, 71), N_SHARD).astype(jnp.int32)
    block_perm = jax.random.permutation(jax.random.fold_in(key, 72), total_blocks).astype(jnp.int32)
    owners = jnp.zeros((total_blocks,), jnp.int32).at[block_perm].set(owner_perm[owner_rank])
    slots = jnp.zeros((total_blocks,), jnp.int32).at[block_perm].set(slot_index.astype(jnp.int32))
    return (owners, slots)


def draw_block_owner(key, part):
    return plan_arrays(key)[0]


def draw_block_slot(key, part):
    return plan_arrays(key)[1]


def symmetric_blocks(key, diag_low, diag_high, reach):
    total_slots = N_SHARD * CAP
    noise = jax.random.uniform(jax.random.fold_in(key, 5), (total_slots, BS, BS), jnp.float32, -reach, reach)
    noise = 0.5 * (noise + jnp.swapaxes(noise, 1, 2))
    diagonal = jnp.exp(jax.random.uniform(jax.random.fold_in(key, 6), (total_slots, BS), jnp.float32, math.log(diag_low), math.log(diag_high)))
    return noise + diagonal[:, :, None] * jnp.eye(BS, dtype=jnp.float32)[None, :, :]


def draw_left_factor(key, part):
    return symmetric_blocks(jax.random.fold_in(key, 11), 2.0, 20.0, 1.7 / BS ** 0.5)


def draw_right_factor(key, part):
    return symmetric_blocks(jax.random.fold_in(key, 12), 2.0, 20.0, 1.7 / BS ** 0.5)


def draw_left_root(key, part):
    return symmetric_blocks(jax.random.fold_in(key, 13), 0.5, 2.0, 1.0 / BS ** 0.5).astype(jnp.bfloat16)


def draw_right_root(key, part):
    return symmetric_blocks(jax.random.fold_in(key, 14), 0.5, 2.0, 1.0 / BS ** 0.5).astype(jnp.bfloat16)


def strengthened(entries, key, source, target, shards_of, factor):
    def block_of(dim):
        return (jnp.arange(entries.shape[dim]) // (entries.shape[dim] // shards_of)).reshape((-1,) + (1,) * (entries.ndim - 1 - dim))

    one_side = jax.random.permutation(key, shards_of)[block_of(target)]
    far = (block_of(target) + shards_of // 2) % shards_of
    return jnp.where((block_of(source) == one_side) | (block_of(source) == far), factor * entries, entries)


def block_scale(own_key, dims, shards, smallest, high):
    factor_of, own = 1.0, jax.random.fold_in(own_key, 6)
    for position, blocks in shards:
        heights = jnp.exp(jax.random.uniform(jax.random.fold_in(own, position), (blocks,), jnp.float32, smallest / len(shards), high / len(shards)))
        factor_of = factor_of * jnp.repeat(heights, dims[position] // blocks).reshape([-1 if axis == position else 1 for axis in range(len(dims))])
    return factor_of


def gaussian(own_key, dims, scale, bound, cuts=(), kind=jnp.bfloat16):
    entries = jax.random.normal(own_key, dims, jnp.float32) * scale
    if len(cuts) > 0:
        entries = block_scale(own_key, dims, cuts, -0.22, 0.18) * entries
    return jnp.clip(entries, min=-bound, max=bound).astype(kind)


def gaussian_with(own_key, dims, spread, most, pieces, heavy, held_as=jnp.bfloat16):
    result = spread * jax.random.normal(own_key, dims, jnp.float32)
    if pieces:
        result = result * block_scale(own_key, dims, pieces, -0.22, 0.18)
    return jnp.clip(strengthened(result, jax.random.fold_in(own_key, 3), *heavy), -most, most).astype(held_as)


def setup_inputs(seed: int = 0) -> dict:
    splits = jax.random.split(jax.random.key(seed), 9)
    hidden_states = gaussian(splits[0], (TOKENS, D), 1.0, 6.0, ((0, 32),))
    latent_grad = gaussian_with(splits[1], (TOKENS, LAT), (0.5 / (TOK_DEV * N_REPLICA * N_SHARD) ** 0.5), 0.15625, ((0, 32),), (0, 1, 32, 2.75))
    left_factor = draw_left_factor(jax.random.fold_in(splits[8], 71), 0)
    right_factor = draw_right_factor(jax.random.fold_in(splits[8], 71), 0)
    left_root = draw_left_root(jax.random.fold_in(splits[8], 71), 0)
    right_root = draw_right_root(jax.random.fold_in(splits[8], 71), 0)
    block_owner = draw_block_owner(jax.random.fold_in(splits[8], 71), 0)
    block_slot = draw_block_slot(jax.random.fold_in(splits[8], 71), 0)
    return dict(hidden_states=hidden_states, latent_grad=latent_grad, left_factor=left_factor, right_factor=right_factor, left_root=left_root, right_root=right_root, block_owner=block_owner, block_slot=block_slot)


decay_rate = 0.95
epsilon = 1e-06

def reference(hidden_states, latent_grad, left_factor, right_factor, left_root, right_root, block_owner, block_slot):
    groups = N_REPLICA * N_SHARD
    inputs = hidden_states.reshape(groups, TOK_DEV, D)
    cotangents = latent_grad.reshape(groups, TOK_DEV, LAT)

    def accumulate(total, pair):
        span_in, span_out = pair
        partial_value = jnp.dot(span_out.T, span_in, preferred_element_type=jnp.float32).astype(jnp.bfloat16)
        partial_value = lax.optimization_barrier(partial_value)
        return (total + partial_value.astype(jnp.float32), None)
    gradient, _ = lax.scan(accumulate, jnp.zeros((LAT, D), jnp.float32), (inputs, cotangents))
    row_blocks = LAT // BS
    col_blocks = D // BS
    count = row_blocks * col_blocks
    blocks = gradient.reshape(row_blocks, BS, col_blocks, BS).transpose(0, 2, 1, 3).reshape(count, BS, BS)
    slot_index = (block_owner * CAP + block_slot).astype(jnp.int32)
    slot_grad = jnp.zeros((N_SHARD * CAP, BS, BS), jnp.float32).at[slot_index].set(blocks)
    high = lax.Precision.HIGHEST
    new_left = decay_rate * left_factor + (1.0 - decay_rate) * jnp.einsum('cik,cjk->cij', slot_grad, slot_grad, precision=high)
    new_right = decay_rate * right_factor + (1.0 - decay_rate) * jnp.einsum('cki,ckj->cij', slot_grad, slot_grad, precision=high)
    rounded = lax.optimization_barrier(slot_grad.astype(jnp.bfloat16)).astype(jnp.float32)
    half_product = jnp.einsum('cik,ckj->cij', left_root.astype(jnp.float32), rounded, precision=high).astype(jnp.bfloat16)
    half_product = lax.optimization_barrier(half_product).astype(jnp.float32)
    shaped = jnp.einsum('cik,ckj->cij', half_product, right_root.astype(jnp.float32), precision=high)
    grad_scale = jnp.sqrt(lax.optimization_barrier(jnp.mean(slot_grad * slot_grad, axis=(1, 2))))
    shaped_scale = jnp.sqrt(lax.optimization_barrier(jnp.mean(shaped * shaped, axis=(1, 2))) + epsilon)
    grafted = shaped * (grad_scale / shaped_scale)[:, None, None]
    chosen = grafted[slot_index]
    update = chosen.reshape(row_blocks, col_blocks, BS, BS).transpose(0, 2, 1, 3).reshape(row_blocks, BS, D)
    return (new_left, new_right, update)
```

```python
import jax
import jax.numpy as jnp
import numpy as np
from jax import lax
from jax.sharding import PartitionSpec as P

D = 7168
LAT = 512
BS = 256

decay_rate = 0.95
epsilon = 1e-06


def bits_of(size):
    return [1 << k for k in range(size.bit_length() - 1)]


def split_columns(col_blocks, parts):
    edges = [round(col_blocks * k / parts) for k in range(parts + 1)]
    return [(edges[k], edges[k + 1]) for k in range(parts)]


def swap(value, axis, mask):
    size = lax.axis_size(axis)
    return lax.ppermute(value, axis, [(k, k ^ mask) for k in range(size)])


def rounded(value):
    return lax.reduce_precision(value, 8, 7)


def halving_orders(replicas, shards):
    shard_bits = [("shard", m) for m in bits_of(shards)]
    replica_bits = [("replica", m) for m in bits_of(replicas)]
    first, second, rest = shard_bits[:1], shard_bits[1:2], shard_bits[2:]
    return (first + second + replica_bits + rest, first + replica_bits + second + rest)


def relative_rows(order, replicas, shards, strip_index):
    devices = replicas * shards
    rows = BS // devices
    position = np.arange(LAT)
    row_in_strip = position % rows
    row_block = position // rows % (LAT // BS)
    steps = position // (rows * (LAT // BS))
    relative = np.zeros_like(position)
    for place, (axis, mask) in enumerate(order):
        bit = steps >> (len(order) - 1 - place) & 1
        relative += bit * mask * (shards if axis == "replica" else 1)
    strip = jnp.asarray(relative, jnp.int32) ^ strip_index
    return jnp.asarray(row_block * BS + row_in_strip, jnp.int32) + strip * rows


def reduce_chunk(order, latent_rows, hidden_part):
    half = latent_rows.shape[0] // 2
    product = lambda rows: rounded(
        jnp.dot(rows, hidden_part, preferred_element_type=jnp.float32)
    ).astype(jnp.bfloat16)
    sent = product(latent_rows[half:])
    received = swap(sent, *order[0])
    kept = product(latent_rows[:half])
    total = kept.astype(jnp.float32) + received.astype(jnp.float32)
    for axis, mask in order[1:]:
        half = total.shape[0] // 2
        received = swap(total[half:].astype(jnp.bfloat16), axis, mask)
        total = total[:half] + received.astype(jnp.float32)
    return total


def local(
    hidden_states,
    latent_grad,
    left_factor,
    right_factor,
    left_root,
    right_root,
    block_owner,
    block_slot,
):
    shards = lax.axis_size("shard")
    replicas = lax.axis_size("replica")
    devices = shards * replicas
    rows = BS // devices
    strip_rows = BS // shards
    row_blocks = LAT // BS
    col_blocks = D // BS
    block_count = row_blocks * col_blocks
    capacity = left_root.shape[0]
    replica = lax.axis_index("replica")
    strip_index = replica * shards + lax.axis_index("shard")

    orders = halving_orders(replicas, shards)
    latent_rows = []
    for order in orders:
        wanted = relative_rows(order, replicas, shards, strip_index)
        pick = (wanted[:, None] == lax.broadcasted_iota(jnp.int32, (LAT, LAT), 1)).astype(
            jnp.bfloat16
        )
        latent_rows.append(
            jnp.einsum(
                "ql,tl->qt", pick, latent_grad, preferred_element_type=jnp.float32
            ).astype(jnp.bfloat16)
        )
    pieces = []
    for number, (start, stop) in enumerate(split_columns(col_blocks, 4)):
        which = number % 2
        pieces.append(
            reduce_chunk(
                orders[which], latent_rows[which], hidden_states[:, start * BS : stop * BS]
            )
        )
    strip = jnp.concatenate(
        [
            piece.astype(jnp.bfloat16)
            .reshape(row_blocks, rows, piece.shape[1] // BS, BS)
            .transpose(0, 2, 1, 3)
            for piece in pieces
        ],
        axis=1,
    ).reshape(block_count, rows * BS)

    flat_slot = block_owner * capacity + block_slot
    owners_iota = lax.broadcasted_iota(jnp.int32, (shards * capacity, block_count), 0)
    matcher = (owners_iota == flat_slot[None, :]).astype(jnp.bfloat16)
    outgoing = jnp.dot(matcher, strip, preferred_element_type=jnp.float32).astype(jnp.bfloat16)
    outgoing = jnp.broadcast_to(
        outgoing.reshape(1, shards, capacity, rows, BS), (replicas, shards, capacity, rows, BS)
    ).reshape(devices, capacity, rows, BS)
    blocks = (
        lax.all_to_all(outgoing, ("replica", "shard"), split_axis=0, concat_axis=0, tiled=True)
        .transpose(1, 0, 2, 3)
        .reshape(capacity, BS, BS)
    )

    part_rows = BS // replicas
    row_start = replica * part_rows
    rows_part = lax.dynamic_slice_in_dim(blocks, row_start, part_rows, 1)
    cols_part = lax.dynamic_slice_in_dim(blocks, row_start, part_rows, 2)
    half_product = jnp.einsum(
        "cik,ckj->cij", left_root, blocks, preferred_element_type=jnp.float32
    )
    coarse = rounded(half_product)
    fine = (half_product - coarse).astype(jnp.bfloat16)
    shaped = jnp.einsum(
        "cik,ckj->cij", coarse.astype(jnp.bfloat16), right_root, preferred_element_type=jnp.float32
    ) + jnp.einsum("cik,ckj->cij", fine, right_root, preferred_element_type=jnp.float32)
    wide = blocks.astype(jnp.float32)
    grad_scale = jnp.sqrt(jnp.mean(wide * wide, axis=(1, 2)))
    shaped_scale = jnp.sqrt(jnp.mean(shaped * shaped, axis=(1, 2)) + epsilon)
    update_blocks = (shaped * (grad_scale / shaped_scale)[:, None, None]).astype(jnp.bfloat16)
    mine = lax.dynamic_index_in_dim(
        update_blocks.reshape(capacity, shards, replicas, rows, BS), replica, 2, keepdims=False
    ).transpose(1, 0, 2, 3)
    mine = jnp.broadcast_to(mine[None], (replicas,) + mine.shape).reshape(
        devices, capacity, rows, BS
    )
    returned = lax.all_to_all(
        mine, ("replica", "shard"), split_axis=0, concat_axis=0, tiled=True
    )
    returned = (
        returned.reshape(replicas, shards * capacity, rows, BS)
        .transpose(1, 0, 2, 3)
        .reshape(shards * capacity, strip_rows * BS)
    )

    new_left = decay_rate * left_factor + (1.0 - decay_rate) * jnp.einsum(
        "cik,cjk->cij", rows_part, blocks, preferred_element_type=jnp.float32
    )
    new_right = decay_rate * right_factor + (1.0 - decay_rate) * jnp.einsum(
        "cki,ckj->cij", cols_part, blocks, preferred_element_type=jnp.float32
    )

    pick_iota = lax.broadcasted_iota(jnp.int32, (block_count, shards * capacity), 1)
    selector = (pick_iota == flat_slot[:, None]).astype(jnp.bfloat16)
    chosen = jnp.dot(selector, returned, preferred_element_type=jnp.float32)
    update = (
        chosen.reshape(row_blocks, col_blocks, strip_rows, BS)
        .transpose(0, 2, 1, 3)
        .reshape(row_blocks, strip_rows, D)
    )
    return (new_left, new_right, update)


def gathered(
    hidden_states,
    latent_grad,
    left_factor,
    right_factor,
    left_root,
    right_root,
    block_owner,
    block_slot,
):
    shards = lax.axis_size("shard")
    replicas = lax.axis_size("replica")
    strip_rows = BS // shards
    row_blocks = LAT // BS
    col_blocks = D // BS
    block_count = row_blocks * col_blocks
    capacity = left_root.shape[0]
    high = lax.Precision.HIGHEST
    tokens_here = latent_grad.shape[0]
    reordered = (
        latent_grad.reshape(tokens_here, row_blocks, shards, strip_rows)
        .transpose(0, 2, 1, 3)
        .reshape(tokens_here, LAT)
    )
    partial_value = jnp.einsum(
        "tl,td->ld", reordered, hidden_states, preferred_element_type=jnp.float32
    ).astype(jnp.bfloat16)
    pieces = partial_value.reshape(LAT, replicas, D // replicas)
    received = lax.all_to_all(pieces, "replica", split_axis=1, concat_axis=1, tiled=True)
    summed = jnp.sum(received, axis=1, dtype=jnp.float32).reshape(
        shards, row_blocks * strip_rows, D // replicas
    )
    shard_total = lax.psum_scatter(summed, "shard", scatter_dimension=0, tiled=True).reshape(
        row_blocks * strip_rows, D // replicas
    )
    gradient_slab = lax.all_gather(shard_total, "replica", axis=1, tiled=True)
    strips = (
        gradient_slab.reshape(row_blocks, strip_rows, col_blocks, BS)
        .transpose(0, 2, 1, 3)
        .reshape(block_count, strip_rows * BS)
    )
    flat_slot = block_owner * capacity + block_slot
    owners_iota = lax.broadcasted_iota(jnp.int32, (shards * capacity, block_count), 0)
    matcher = (owners_iota == flat_slot[None, :]).astype(jnp.float32)
    outgoing = jnp.dot(matcher, strips, precision=high, preferred_element_type=jnp.float32).reshape(
        shards, capacity, strip_rows, BS
    )
    blocks = (
        lax.all_to_all(
            outgoing.astype(jnp.bfloat16), "shard", split_axis=0, concat_axis=2, tiled=True
        )
        .astype(outgoing.dtype)
        .reshape(capacity, BS, BS)
    )
    part_rows = BS // replicas
    row_start = lax.axis_index("replica") * part_rows
    rows_part = lax.dynamic_slice_in_dim(blocks, row_start, part_rows, 1)
    cols_part = lax.dynamic_slice_in_dim(blocks, row_start, part_rows, 2)
    new_left = decay_rate * left_factor + (1.0 - decay_rate) * jnp.einsum(
        "cik,cjk->cij", rows_part, blocks, precision=high
    )
    new_right = decay_rate * right_factor + (1.0 - decay_rate) * jnp.einsum(
        "cki,ckj->cij", cols_part, blocks, precision=high
    )
    half_product = jnp.einsum(
        "cik,ckj->cij", left_root, blocks.astype(jnp.bfloat16), preferred_element_type=jnp.float32
    ).astype(jnp.bfloat16)
    shaped = jnp.einsum(
        "cik,ckj->cij", half_product, right_root, preferred_element_type=jnp.float32
    )
    grad_scale = jnp.sqrt(jnp.mean(blocks * blocks, axis=(1, 2)))
    shaped_scale = jnp.sqrt(jnp.mean(shaped * shaped, axis=(1, 2)) + epsilon)
    update_blocks = shaped * (grad_scale / shaped_scale)[:, None, None]
    returned = lax.all_to_all(
        update_blocks.reshape(capacity, shards, strip_rows, BS),
        "shard",
        split_axis=1,
        concat_axis=1,
        tiled=True,
    )
    pick_iota = lax.broadcasted_iota(jnp.int32, (block_count, capacity * shards), 1)
    slot_key = block_slot * shards + block_owner
    selector = (pick_iota == slot_key[:, None]).astype(jnp.float32)
    chosen_rows = jnp.dot(
        selector,
        returned.reshape(capacity * shards, strip_rows * BS),
        precision=high,
        preferred_element_type=jnp.float32,
    )
    update = (
        chosen_rows.reshape(row_blocks, col_blocks, strip_rows, BS)
        .transpose(0, 2, 1, 3)
        .reshape(row_blocks, strip_rows, D)
    )
    return (new_left, new_right, update)


def solution(mesh):
    replicas, shards = mesh.shape["replica"], mesh.shape["shard"]
    powers = all(n & (n - 1) == 0 for n in (replicas, shards))
    body = local if powers and BS % (replicas * shards) == 0 else gathered
    placed = (
        P(("replica", "shard"), None),
        P(("replica", "shard"), None),
        P("shard", "replica", None),
        P("shard", "replica", None),
        P("shard", None, None),
        P("shard", None, None),
        P(),
        P(),
    )
    return jax.shard_map(
        body,
        mesh=mesh,
        in_specs=placed,
        out_specs=(
            P("shard", "replica", None),
            P("shard", "replica", None),
            P(None, "shard", None),
        ),
        check_vma=False,
    )
```

```python
import jax
import jax.numpy as jnp
import numpy as np
from jax import lax
from jax.sharding import PartitionSpec as P

D = 7168
LAT = 512
BS = 256

decay_rate = 0.95
epsilon = 1e-06

CHUNKS = (("x", 7), ("y", 7), ("x", 7), ("y", 7))


def bits_of(size):
    return [1 << k for k in range(size.bit_length() - 1)]


def swap(value, axis, mask):
    size = lax.axis_size(axis)
    return lax.ppermute(value, axis, [(k, k ^ mask) for k in range(size)])


def rounded(value):
    return lax.reduce_precision(value, 8, 7)


def halving_steps(replicas, shards):
    shard_bits = [("shard", m) for m in bits_of(shards)]
    replica_bits = [("replica", m) for m in bits_of(replicas)]
    return shard_bits[:2] + replica_bits + shard_bits[2:]


def relative_rows(steps, replicas, shards, strip_index, first, count):
    devices = replicas * shards
    row_blocks = LAT // BS
    position = np.arange(devices * row_blocks * count)
    taken = position // (count * row_blocks)
    relative = np.zeros_like(position)
    for place, (axis, mask) in enumerate(steps):
        bit = taken >> (len(steps) - 1 - place) & 1
        relative += bit * mask * (shards if axis == "replica" else 1)
    strip = jnp.asarray(relative, jnp.int32) ^ strip_index
    base = position // count % row_blocks * BS + first * devices + position % count
    return jnp.asarray(base, jnp.int32) + strip * count


def products(steps, latent_rows, hidden_part):
    half = latent_rows.shape[0] // 2

    def product(rows):
        value = jnp.dot(rows, hidden_part, preferred_element_type=jnp.float32)
        return rounded(value).astype(jnp.bfloat16)

    received = swap(product(latent_rows[half:]), *steps[0])
    kept = product(latent_rows[:half])
    return kept.astype(jnp.float32) + received.astype(jnp.float32)


def reduce_chunk(steps, places, total):
    left = list(range(1, len(steps)))
    for place in places:
        at = left.index(place)
        left.remove(place)
        cut = total.reshape(1 << at, 2, -1, total.shape[-1])
        received = swap(cut[:, 1].astype(jnp.bfloat16), *steps[place])
        total = (cut[:, 0] + received.astype(jnp.float32)).reshape(-1, total.shape[-1])
    return total


def chunk_edges(col_blocks):
    weights = [weight for _, weight in CHUNKS]
    ends = np.round(np.cumsum([0] + weights) * col_blocks / sum(weights)).astype(int)
    return [
        (kind, int(a), int(b)) for (kind, _), a, b in zip(CHUNKS, ends[:-1], ends[1:]) if b > a
    ]


def local(
    hidden_states,
    latent_grad,
    left_factor,
    right_factor,
    left_root,
    right_root,
    block_owner,
    block_slot,
):
    shards = lax.axis_size("shard")
    replicas = lax.axis_size("replica")
    devices = shards * replicas
    rows = BS // devices
    strip_rows = BS // shards
    row_blocks = LAT // BS
    col_blocks = D // BS
    block_count = row_blocks * col_blocks
    capacity = left_root.shape[0]
    per = capacity // replicas
    own = per * replicas
    shared = capacity - own
    held = per + shared
    replica = lax.axis_index("replica")
    strip_index = replica * shards + lax.axis_index("shard")
    everyone = ("replica", "shard")

    flat_slot = block_owner * capacity + block_slot
    wanted = np.array(
        [
            [
                [o * capacity + (y * per + k if k < per else own + k - per) for k in range(held)]
                for o in range(shards)
            ]
            for y in range(replicas)
        ],
        np.int32,
    ).reshape(-1)
    matcher = (jnp.asarray(wanted)[:, None] == flat_slot[None, :]).astype(jnp.bfloat16)

    steps = halving_steps(replicas, shards)
    rest = list(range(2 + len(bits_of(replicas)), len(steps)))
    across = list(range(2, 2 + len(bits_of(replicas))))
    kinds = {
        "x": [1] + across + rest,
        "y": across + [1] + rest,
        "z": rest + [1] + across,
    }
    row_of = relative_rows(steps, replicas, shards, strip_index, 0, rows)
    pick = (row_of[:, None] == jnp.arange(LAT, dtype=jnp.int32)[None, :]).astype(jnp.bfloat16)
    latent_rows = jnp.einsum(
        "ql,tl->qt", pick, latent_grad, preferred_element_type=jnp.float32
    ).astype(jnp.bfloat16)
    pieces = []
    for kind, start, stop in chunk_edges(col_blocks):
        total = products(steps, latent_rows, hidden_states[:, start * BS : stop * BS])
        pieces.append(
            reduce_chunk(steps, kinds[kind], total)
            .astype(jnp.bfloat16)
            .reshape(row_blocks, rows, stop - start, BS)
            .transpose(0, 2, 1, 3)
        )
    strip = jnp.concatenate(pieces, axis=1).reshape(block_count, rows * BS)
    outgoing = (
        jnp.dot(matcher, strip, preferred_element_type=jnp.float32)
        .astype(jnp.bfloat16)
        .reshape(devices, held, rows, BS)
    )
    incoming = lax.all_to_all(outgoing, everyone, split_axis=0, concat_axis=0, tiled=True)
    blocks = incoming.transpose(1, 0, 2, 3).reshape(held, BS, BS)

    def mine_of(roots):
        return jnp.concatenate(
            [lax.dynamic_slice_in_dim(roots, replica * per, per, 0), roots[own:]], axis=0
        )

    half_product = jnp.einsum(
        "cik,ckj->cij", mine_of(left_root), blocks, preferred_element_type=jnp.float32
    )
    coarse = rounded(half_product)
    fine = (half_product - coarse).astype(jnp.bfloat16)
    right = mine_of(right_root)
    shaped = jnp.einsum(
        "cik,ckj->cij", coarse.astype(jnp.bfloat16), right, preferred_element_type=jnp.float32
    ) + jnp.einsum("cik,ckj->cij", fine, right, preferred_element_type=jnp.float32)
    wide = blocks.astype(jnp.float32)
    grad_scale = jnp.sqrt(jnp.mean(wide * wide, axis=(1, 2)))
    shaped_scale = jnp.sqrt(jnp.mean(shaped * shaped, axis=(1, 2)) + epsilon)
    update_blocks = (shaped * (grad_scale / shaped_scale)[:, None, None]).astype(jnp.bfloat16)
    whole = (
        update_blocks[:per]
        .reshape(per, shards, strip_rows, BS)
        .transpose(1, 0, 2, 3)
        .reshape(shards, per * strip_rows, BS)
    )
    split = lax.dynamic_index_in_dim(
        update_blocks[per:].reshape(shared, shards, replicas, rows, BS), replica, 2, keepdims=False
    )
    split = split.transpose(1, 0, 2, 3).reshape(shards, shared * rows, BS)
    leaving = jnp.concatenate([whole, split], axis=1)
    leaving = jnp.broadcast_to(leaving[None], (replicas,) + leaving.shape).reshape(
        (devices,) + leaving.shape[1:]
    )
    returned = lax.all_to_all(leaving, everyone, split_axis=0, concat_axis=0, tiled=True)

    relative = [blocks[:per]] + [swap(blocks[:per], "replica", k) for k in range(1, replicas)]
    relative = jnp.stack(relative)
    every = jnp.concatenate(
        [lax.dynamic_index_in_dim(relative, replica ^ k, 0, keepdims=False) for k in range(replicas)]
        + [blocks[per:]],
        axis=0,
    )
    part_rows = BS // replicas
    row_start = replica * part_rows
    rows_part = lax.dynamic_slice_in_dim(every, row_start, part_rows, 1)
    cols_part = lax.dynamic_slice_in_dim(every, row_start, part_rows, 2)
    new_left = decay_rate * left_factor + (1.0 - decay_rate) * jnp.einsum(
        "cik,cjk->cij", rows_part, every, preferred_element_type=jnp.float32
    )
    new_right = decay_rate * right_factor + (1.0 - decay_rate) * jnp.einsum(
        "cki,ckj->cij", cols_part, every, preferred_element_type=jnp.float32
    )

    whole = returned[:, : per * strip_rows].reshape(devices * per, strip_rows * BS)
    split = (
        returned[:, per * strip_rows :]
        .reshape(replicas, shards, shared, rows, BS)
        .transpose(1, 2, 0, 3, 4)
        .reshape(shards * shared, strip_rows * BS)
    )
    source = jnp.where(
        block_slot < own,
        (block_slot // max(per, 1) * shards + block_owner) * per + block_slot % max(per, 1),
        devices * per + block_owner * shared + block_slot - own,
    )
    places_iota = jnp.arange(devices * per + shards * shared, dtype=jnp.int32)
    selector = (places_iota[None, :] == source[:, None]).astype(jnp.bfloat16)
    chosen = jnp.dot(
        selector, jnp.concatenate([whole, split], axis=0), preferred_element_type=jnp.float32
    )
    update = (
        chosen.reshape(row_blocks, col_blocks, strip_rows, BS)
        .transpose(0, 2, 1, 3)
        .reshape(row_blocks, strip_rows, D)
    )
    return (new_left, new_right, update)


def gathered(
    hidden_states,
    latent_grad,
    left_factor,
    right_factor,
    left_root,
    right_root,
    block_owner,
    block_slot,
):
    shards = lax.axis_size("shard")
    replicas = lax.axis_size("replica")
    strip_rows = BS // shards
    row_blocks = LAT // BS
    col_blocks = D // BS
    block_count = row_blocks * col_blocks
    capacity = left_root.shape[0]
    high = lax.Precision.HIGHEST
    tokens_here = latent_grad.shape[0]
    reordered = (
        latent_grad.reshape(tokens_here, row_blocks, shards, strip_rows)
        .transpose(0, 2, 1, 3)
        .reshape(tokens_here, LAT)
    )
    partial_value = jnp.einsum(
        "tl,td->ld", reordered, hidden_states, preferred_element_type=jnp.float32
    ).astype(jnp.bfloat16)
    pieces = partial_value.reshape(LAT, replicas, D // replicas)
    received = lax.all_to_all(pieces, "replica", split_axis=1, concat_axis=1, tiled=True)
    summed = jnp.sum(received, axis=1, dtype=jnp.float32).reshape(
        shards, row_blocks * strip_rows, D // replicas
    )
    shard_total = lax.psum_scatter(summed, "shard", scatter_dimension=0, tiled=True).reshape(
        row_blocks * strip_rows, D // replicas
    )
    gradient_slab = lax.all_gather(shard_total, "replica", axis=1, tiled=True)
    strips = (
        gradient_slab.reshape(row_blocks, strip_rows, col_blocks, BS)
        .transpose(0, 2, 1, 3)
        .reshape(block_count, strip_rows * BS)
    )
    flat_slot = block_owner * capacity + block_slot
    owners_iota = lax.broadcasted_iota(jnp.int32, (shards * capacity, block_count), 0)
    matcher = (owners_iota == flat_slot[None, :]).astype(jnp.float32)
    outgoing = jnp.dot(matcher, strips, precision=high, preferred_element_type=jnp.float32).reshape(
        shards, capacity, strip_rows, BS
    )
    blocks = (
        lax.all_to_all(
            outgoing.astype(jnp.bfloat16), "shard", split_axis=0, concat_axis=2, tiled=True
        )
        .astype(outgoing.dtype)
        .reshape(capacity, BS, BS)
    )
    part_rows = BS // replicas
    row_start = lax.axis_index("replica") * part_rows
    rows_part = lax.dynamic_slice_in_dim(blocks, row_start, part_rows, 1)
    cols_part = lax.dynamic_slice_in_dim(blocks, row_start, part_rows, 2)
    new_left = decay_rate * left_factor + (1.0 - decay_rate) * jnp.einsum(
        "cik,cjk->cij", rows_part, blocks, precision=high
    )
    new_right = decay_rate * right_factor + (1.0 - decay_rate) * jnp.einsum(
        "cki,ckj->cij", cols_part, blocks, precision=high
    )
    half_product = jnp.einsum(
        "cik,ckj->cij", left_root, blocks.astype(jnp.bfloat16), preferred_element_type=jnp.float32
    ).astype(jnp.bfloat16)
    shaped = jnp.einsum(
        "cik,ckj->cij", half_product, right_root, preferred_element_type=jnp.float32
    )
    grad_scale = jnp.sqrt(jnp.mean(blocks * blocks, axis=(1, 2)))
    shaped_scale = jnp.sqrt(jnp.mean(shaped * shaped, axis=(1, 2)) + epsilon)
    update_blocks = shaped * (grad_scale / shaped_scale)[:, None, None]
    returned = lax.all_to_all(
        update_blocks.reshape(capacity, shards, strip_rows, BS),
        "shard",
        split_axis=1,
        concat_axis=1,
        tiled=True,
    )
    pick_iota = lax.broadcasted_iota(jnp.int32, (block_count, capacity * shards), 1)
    slot_key = block_slot * shards + block_owner
    selector = (pick_iota == slot_key[:, None]).astype(jnp.float32)
    chosen_rows = jnp.dot(
        selector,
        returned.reshape(capacity * shards, strip_rows * BS),
        precision=high,
        preferred_element_type=jnp.float32,
    )
    update = (
        chosen_rows.reshape(row_blocks, col_blocks, strip_rows, BS)
        .transpose(0, 2, 1, 3)
        .reshape(row_blocks, strip_rows, D)
    )
    return (new_left, new_right, update)


def solution(mesh):
    replicas, shards = mesh.shape["replica"], mesh.shape["shard"]
    powers = all(n & (n - 1) == 0 for n in (replicas, shards))
    body = local if powers and BS % (replicas * shards) == 0 else gathered
    placed = (
        P(("replica", "shard"), None),
        P(("replica", "shard"), None),
        P("shard", "replica", None),
        P("shard", "replica", None),
        P("shard", None, None),
        P("shard", None, None),
        P(),
        P(),
    )
    return jax.shard_map(
        body,
        mesh=mesh,
        in_specs=placed,
        out_specs=(
            P("shard", "replica", None),
            P("shard", "replica", None),
            P(None, "shard", None),
        ),
        check_vma=False,
    )
```
